32 devices in a mesh: pat: 8 (over y, x, core), src: 4 (over z).
Axes of the slice: x: 2, y: 2, z: 4, core: 2. Of those that a mesh axis runs over, the one named last changes fastest.
Arguments:
- patterns: bfloat16 [8192, 12288], P('src', 'pat'), may hold values from -6 to 6
- left_factors: bfloat16 [3, 8, 512, 1024], P(None, 'src', 'pat'), may hold values from -0.125 to 0.125
- right_factors: bfloat16 [3, 8, 512, 1024], P(None, 'src', 'pat'), may hold values from -0.1875 to 0.1875
- ranks: int32 [3, 8], replicated, may hold values from 128 to 512, as said below
- source_slot_tile: int32 [8], replicated, may hold values from 0 to 7, each once
Outputs:
- potentials: float32 [3072, 12288], P('src', 'pat')
The draws below stay inside these ranges and needn't reach their ends.
Inputs may be any that keep to these rules, and one draw needn't show every extreme that they name: `ranks`: some tile has rank exactly 512 and some exactly 128. `source_slot_tile`: every source tile is held by exactly one slot.
All inputs are finite; a program needn't handle non-finite values.
Results may differ from the reference program's by a relative error of at most 0.01.
Values may be sent and summed in bfloat16 or wider, within the bound.
No kernel may reach another device: no remote copies, remote signals or barrier semaphores. Data moves between devices by JAX's collectives and lax.ppermute only.
A program may use at most 576 MiB of HBM per device.

```python
import jax
import jax.numpy as jnp
from jax import lax

TILE_ROWS = 1024
LARGEST_RANK = 512
SMALLEST_RANK = 128
TARGET_ROWS = 3
SLOT_DEV = 2
SOURCE_SLOTS = 8
CURRENT_PATTERNS = 12288
N_SRC = 4


def draw_ranks(key, part):
    first_factor, second_factor = jax.random.split(key)
    value_entries = jax.random.randint(first_factor, (TARGET_ROWS * SOURCE_SLOTS,), SMALLEST_RANK, LARGEST_RANK + 1)
    picked_slots = jax.random.permutation(second_factor, TARGET_ROWS * SOURCE_SLOTS)
    placement_list = jnp.arange(TARGET_ROWS * SOURCE_SLOTS)
    value_entries = jnp.where(placement_list == picked_slots[0], LARGEST_RANK, value_entries)
    value_entries = jnp.where(placement_list == picked_slots[1], SMALLEST_RANK, value_entries)
    return value_entries.reshape(TARGET_ROWS, SOURCE_SLOTS).astype(jnp.int32)


def shard_levels(own_key, shape, cuts, smallest, high):
    gain = 1.0
    for dim, parts in cuts:
        heights = jax.random.uniform(jax.random.fold_in(jax.random.fold_in(own_key, 6), dim), (parts,), jnp.float32, smallest / len(cuts), high / len(cuts))
        gain = gain * jnp.repeat(jnp.exp(heights), shape[dim] // parts).reshape((-1,) + (1,) * (len(shape) - 1 - dim))
    return gain


def centred(stream_key, extent, spread, bound, cuts=(), kind=jnp.bfloat16):
    array = spread * jax.random.normal(stream_key, extent, jnp.float32)
    if cuts:
        array = array * shard_levels(stream_key, extent, cuts, -0.22, 0.18)
    return jnp.clip(array, -bound, bound).astype(kind)


def setup_inputs(seed: int = 0) -> dict:
    streams_of = jax.random.split(jax.random.key(seed), 6)
    patterns = centred(streams_of[0], (SOURCE_SLOTS * TILE_ROWS, CURRENT_PATTERNS), 1.0, 6.0, ((0, 4), (1, 8)))
    left_factors = centred(streams_of[1], (TARGET_ROWS, SOURCE_SLOTS, LARGEST_RANK, TILE_ROWS), (SOURCE_SLOTS * (SMALLEST_RANK + LARGEST_RANK) // 2) ** -0.5, 0.125, ((1, 4), (2, 8)))
    right_factors = centred(streams_of[2], (TARGET_ROWS, SOURCE_SLOTS, LARGEST_RANK, TILE_ROWS), TILE_ROWS ** -0.5, 0.1875, ((1, 4), (2, 8)))
    ranks = draw_ranks(jax.random.fold_in(streams_of[5], 71), 0)
    source_slot_tile = jax.random.permutation(streams_of[4], SOURCE_SLOTS).astype(jnp.int32)
    return dict(patterns=patterns, left_factors=left_factors, right_factors=right_factors, ranks=ranks, source_slot_tile=source_slot_tile)


def reference(patterns, left_factors, right_factors, ranks, source_slot_tile):
    rank_width = patterns.shape[1]
    slab_pieces = patterns.reshape(SOURCE_SLOTS, TILE_ROWS, rank_width)
    rank_slot = ranks[:, source_slot_tile]
    columns = jnp.arange(LARGEST_RANK, dtype=jnp.int32)

    def group_term(group, total):
        accum = jnp.zeros((TARGET_ROWS, TILE_ROWS, rank_width), jnp.float32)
        for inner in range(SLOT_DEV):
            slot = (group * SLOT_DEV + inner).astype(jnp.int32)
            vpart = lax.dynamic_index_in_dim(right_factors, slot, 1, keepdims=False)
            upart = lax.dynamic_index_in_dim(left_factors, slot, 1, keepdims=False)
            slab = lax.dynamic_index_in_dim(slab_pieces, slot, 0, keepdims=False)
            rank_now = lax.dynamic_index_in_dim(rank_slot, slot, 1, keepdims=False)
            coef = jnp.einsum("trb,bp->trp", vpart.astype(jnp.float32), slab.astype(jnp.float32))
            live = columns[None, :] < rank_now[:, None]
            coef = jnp.where(live[:, :, None], coef, 0.0).astype(jnp.bfloat16)
            accum = accum + jnp.einsum("trb,trp->tbp", upart.astype(jnp.float32), coef.astype(jnp.float32))
        rounded = lax.optimization_barrier(accum.astype(jnp.bfloat16))
        return total + rounded.astype(jnp.float32)

    total = lax.fori_loop(0, N_SRC, group_term, jnp.zeros((TARGET_ROWS, TILE_ROWS, rank_width), jnp.float32))
    return total.reshape(TARGET_ROWS * TILE_ROWS, rank_width)
```

```python
import functools
import math

import jax
import jax.numpy as jnp
from jax import lax
from jax.experimental import pallas as pl
from jax.experimental.pallas import tpu as pltpu
from jax.sharding import PartitionSpec as P

CHUNKS = 2
ANY = pl.BlockSpec(memory_space=pl.ANY)
SMEM = pl.BlockSpec(memory_space=pltpu.SMEM)
VMEM_LIMIT = 48 * 1024 * 1024


def coef_kernel(order, targets, lane_xor, ranks, tiles, *refs):
    *pieces, x_ref, out_ref, v_all, sem = refs
    slot, column = pl.program_id(0), pl.program_id(1)
    slots, count, _ = v_all.shape
    me = lax.axis_index("src")
    size = lax.axis_size("src")
    target = jnp.where(2 * me < size, targets - 1 - order, order)

    def copies(which):
        start = 0
        for piece in pieces:
            rows = piece.shape[1]
            yield pltpu.make_async_copy(
                piece.at[which], v_all.at[which, pl.ds(start, rows)], sem.at[which]
            )
            start += rows

    @pl.when((slot == 0) & (column == 0))
    def _():
        for which in range(slots):
            for copy in copies(which):
                copy.start()

    for which in range(slots):

        @pl.when((slot == which) & (column == 0))
        def _(which=which):
            for copy in copies(which):
                copy.wait()

    rank = ranks[target, tiles[me * slots + slot]]
    value = jnp.dot(v_all[slot], x_ref[...], preferred_element_type=jnp.float32)
    row = lax.broadcasted_iota(jnp.int32, value.shape, 0)
    if lane_xor:
        row = row ^ (lax.axis_index("pat") * lane_xor)
    out_ref[0] = jnp.where(row < rank, value, 0.0).astype(out_ref.dtype)


def coef_call(order, targets, lane_xor, ranks, tiles, pieces, patterns, chunk, width):
    slots, _, tile = pieces[0].shape
    count = sum(piece.shape[1] for piece in pieces)
    block = math.gcd(width, 512) if width % 384 else 384
    steps = width // block
    flops = 2 * slots * count * tile * width
    return pl.pallas_call(
        functools.partial(coef_kernel, order, targets, lane_xor),
        out_shape=jax.ShapeDtypeStruct((slots, count, width), jnp.bfloat16),
        grid=(slots, steps),
        in_specs=[SMEM, SMEM]
        + [ANY] * len(pieces)
        + [pl.BlockSpec((tile, block), lambda s, c: (s, chunk * steps + c))],
        out_specs=pl.BlockSpec((1, count, block), lambda s, c: (s, 0, c)),
        scratch_shapes=[
            pltpu.VMEM((slots, count, tile), jnp.bfloat16),
            pltpu.SemaphoreType.DMA((slots,)),
        ],
        compiler_params=pltpu.CompilerParams(vmem_limit_bytes=VMEM_LIMIT),
        cost_estimate=pl.CostEstimate(
            flops=flops,
            bytes_accessed=2 * slots * (count * tile + tile * width + count * width),
            transcendentals=0,
        ),
        name=f"coef_{order}_{chunk}",
    )(ranks, tiles, *pieces, patterns)


def pack_kernel(*refs):
    *pieces, out_ref, sem = refs
    copies = []
    start = 0
    for piece in pieces:
        rows = piece.shape[1]
        copies.append(
            pltpu.make_async_copy(piece, out_ref.at[:, pl.ds(start, rows)], sem)
        )
        start += rows
    for copy in copies:
        copy.start()
    for copy in copies:
        copy.wait()


def pack_call(pieces, order):
    if len(pieces) == 1:
        return pieces[0]
    slots, _, tile = pieces[0].shape
    count = sum(piece.shape[1] for piece in pieces)
    return pl.pallas_call(
        pack_kernel,
        out_shape=jax.ShapeDtypeStruct((slots, count, tile), jnp.bfloat16),
        in_specs=[ANY] * len(pieces),
        out_specs=pl.BlockSpec(memory_space=pltpu.VMEM),
        scratch_shapes=[pltpu.SemaphoreType.DMA],
        compiler_params=pltpu.CompilerParams(vmem_limit_bytes=VMEM_LIMIT),
        cost_estimate=pl.CostEstimate(
            flops=0, bytes_accessed=4 * slots * count * tile, transcendentals=0
        ),
        name=f"pack_{order}",
    )(*pieces)


def block_kernel(mode, step, targets, strip, counts, adds, aliased, *refs):
    total_pieces = sum(counts)
    left = refs[:total_pieces]
    coef = refs[total_pieces : total_pieces + len(counts)]
    rest = refs[total_pieces + len(counts) :]
    arrived = rest[:adds]
    out_ref, l_all, c_all, l_sem, c_sem = rest[adds + aliased :]
    groups = []
    for count in counts:
        groups.append(left[:count])
        left = left[count:]
    me = lax.axis_index("src")
    size = lax.axis_size("src")
    tile = groups[0][0].shape[2]
    slots = c_all.shape[1]
    rows = out_ref.shape[0]
    strips = rows // strip
    low = 2 * me < size
    up = size - step + me
    down = step - 1 - (size - 1 - me)
    edge = jnp.where(low, size - 1, 0)
    if mode == "own":
        block = me
    elif mode == "up":
        block = jnp.where(up < size, up, edge)
    elif mode == "down":
        block = jnp.where(down >= 0, down, edge)
    else:
        block = jnp.where(low & (up < size), up, jnp.where((~low) & (down >= 0), down, edge))

    def place(index):
        first = block * rows + index * strip
        target = first // tile
        return jnp.where(low, targets - 1 - target, target), first % tile

    def left_copies(index, order, start):
        begin = 0
        for piece in groups[order]:
            height = piece.shape[1]
            yield pltpu.make_async_copy(
                piece.at[:, :, pl.ds(pl.multiple_of(start, 128), strip)],
                l_all.at[index, :, pl.ds(begin, height)],
                l_sem.at[index],
            )
            begin += height

    def coef_copy(order):
        return pltpu.make_async_copy(coef[order], c_all.at[order], c_sem.at[order])

    orders = len(groups)
    places = [place(index) for index in range(strips)]
    for order in range(orders):
        needed = functools.reduce(jnp.logical_or, [at == order for at, _ in places])

        @pl.when(needed)
        def _(order=order):
            coef_copy(order).start()

        for index, (at, start) in enumerate(places):

            @pl.when(at == order)
            def _(index=index, order=order, start=start):
                for copy in left_copies(index, order, start):
                    copy.start()

    for order in range(orders):
        needed = functools.reduce(jnp.logical_or, [at == order for at, _ in places])

        @pl.when(needed)
        def _(order=order):
            coef_copy(order).wait()

    for index, (at, start) in enumerate(places):
        for order in range(orders):

            @pl.when(at == order)
            def _(index=index, order=order, start=start):
                for copy in left_copies(index, order, start):
                    copy.wait()

    @pl.loop(0, strips)
    def _(index):
        at, _ = place(index)
        at = jnp.clip(at, 0, orders - 1)
        span = pl.ds(pl.multiple_of(index * strip, strip), strip)
        value = jnp.zeros((strip, out_ref.shape[1]), jnp.float32)
        for slot in range(slots):
            value = value + lax.dot_general(
                l_all[index, slot],
                c_all[at, slot],
                (((0,), (0,)), ((), ())),
                preferred_element_type=jnp.float32,
            )
        for extra in arrived:
            value = value + extra[span].astype(jnp.float32)
        out_ref[span] = value.astype(out_ref.dtype)


def block_call(mode, step, targets, groups, coef, arrived, rows, chunk, whole=None, chunks=1):
    slots, count, width = coef[0].shape
    tile = groups[0][0].shape[2]
    strip = math.gcd(rows, tile)
    final = mode == "own"
    counts = tuple(len(group) for group in groups)
    operands = [piece for group in groups for piece in group] + list(coef) + list(arrived)
    in_specs = [ANY] * (sum(counts) + len(coef)) + [
        pl.BlockSpec((rows, width), lambda _: (0, 0)) for _ in arrived
    ]
    aliases = {}
    if final and whole is not None:
        aliases = {len(operands): 0}
        operands.append(whole)
        in_specs.append(ANY)
    if final:
        out_shape = jax.ShapeDtypeStruct((rows, width * chunks), jnp.float32)
        out_spec = pl.BlockSpec((rows, width), lambda _: (0, chunk))
    else:
        out_shape = jax.ShapeDtypeStruct((rows, width), jnp.bfloat16)
        out_spec = pl.BlockSpec((rows, width), lambda _: (0, 0))
    return pl.pallas_call(
        functools.partial(
            block_kernel, mode, step, targets, strip, counts, len(arrived), len(aliases)
        ),
        out_shape=out_shape,
        grid=(1,),
        in_specs=in_specs,
        out_specs=out_spec,
        scratch_shapes=[
            pltpu.VMEM((rows // strip, slots, count, strip), jnp.bfloat16),
            pltpu.VMEM((len(coef), slots, count, width), jnp.bfloat16),
            pltpu.SemaphoreType.DMA((rows // strip,)),
            pltpu.SemaphoreType.DMA((len(coef),)),
        ],
        input_output_aliases=aliases,
        compiler_params=pltpu.CompilerParams(vmem_limit_bytes=VMEM_LIMIT),
        cost_estimate=pl.CostEstimate(
            flops=2 * rows * width * slots * count,
            bytes_accessed=2 * (slots * count * (rows + 2 * width) + 3 * rows * width),
            transcendentals=0,
        ),
        name=f"block_{mode}_{step}_{chunk}",
    )(*operands)


def gather(shard, first, second):
    size = lax.axis_size("pat")

    def swap(value, mask):
        return lax.ppermute(value, "pat", [(at, at ^ mask) for at in range(size)])

    near = swap(shard, first)
    side = swap(shard, second)
    far = swap(near, second)
    mine = {0: shard, first: near, second: side, first ^ second: far}
    pieces = dict(mine)
    for mask, value in mine.items():
        pieces[mask ^ 1] = swap(value, 1)
    return [pieces[mask] for mask in range(size)]


def body(patterns, left_factors, right_factors, ranks, source_slot_tile):
    targets, slots, rank_cols, tile = left_factors.shape
    size = lax.axis_size("src")
    pats = lax.axis_size("pat")
    me = lax.axis_index("src")
    low = 2 * me < size
    rows = targets * tile // size
    width = patterns.shape[1] // CHUNKS
    lane_xor = rank_cols if pats == 8 else 0

    rights, lefts = [], []
    for order in range(targets):
        target = jnp.where(low, targets - 1 - order, order)
        right = lax.dynamic_index_in_dim(right_factors, target, 0, keepdims=False)
        left = lax.dynamic_index_in_dim(left_factors, target, 0, keepdims=False)
        if pats == 8:
            rights.append(gather(right, 2, 4))
            lefts.append(gather(left, 4, 2))
        else:
            rights.append([lax.all_gather(right, "pat", axis=1, tiled=True)])
            lefts.append([lax.all_gather(left, "pat", axis=1, tiled=True)])

    coef = [
        [
            coef_call(order, targets, lane_xor, ranks, source_slot_tile, rights[order], patterns, chunk, width)
            for chunk in range(CHUNKS)
        ]
        for order in range(targets)
    ]
    packed = [[pack_call(lefts[order], order)] for order in range(targets)]

    above = [None] * CHUNKS
    below = [None] * CHUNKS
    for step in range(1, size):
        up_pairs = [(at, at + 1) for at in range(step)]
        down_pairs = [(size - 1 - at, size - 2 - at) for at in range(step)]
        for chunk in range(CHUNKS):
            here = [coef[order][chunk] for order in range(targets)]
            if 2 * step <= size:
                used = targets - (size - step) * rows // tile
                groups = (lefts if step == 1 else packed)[:used]
                arrived = [] if step == 1 else [above[chunk], below[chunk]]
                up = down = block_call("both", step, targets, groups, here[:used], arrived, rows, chunk)
            else:
                up = block_call("up", step, targets, packed, here, [above[chunk]], rows, chunk)
                down = block_call("down", step, targets, packed, here, [below[chunk]], rows, chunk)
            above[chunk] = lax.ppermute(up, "src", up_pairs)
            below[chunk] = lax.ppermute(down, "src", down_pairs)
    out = None
    for chunk in range(CHUNKS):
        here = [coef[order][chunk] for order in range(targets)]
        out = block_call(
            "own", 0, targets, packed, here, [above[chunk], below[chunk]], rows, chunk, out, CHUNKS
        )
    return out


def solution(mesh):
    in_specs = (P("src", "pat"), P(None, "src", "pat", None), P(None, "src", "pat", None), P(), P())
    out_specs = P("src", "pat")
    return jax.shard_map(body, mesh=mesh, in_specs=in_specs, out_specs=out_specs, check_vma=False)
```

```python
import functools
import math

import jax
import jax.numpy as jnp
from jax import lax
from jax.experimental import pallas as pl
from jax.experimental.pallas import tpu as pltpu
from jax.sharding import PartitionSpec as P

HBM = pl.BlockSpec(memory_space=pltpu.MemorySpace.HBM)
SMEM = pl.BlockSpec(memory_space=pltpu.MemorySpace.SMEM)


def place():
    me, size = lax.axis_index("src"), lax.axis_size("src")
    return me, size, 2 * me < size


def block_of(mode, step):
    me, size, low = place()
    up = size - step + me
    down = step - 1 - (size - 1 - me)
    edge = jnp.where(low, size - 1, 0)
    up = jnp.where(up < size, up, edge)
    down = jnp.where(down >= 0, down, edge)
    if mode == "own":
        return me
    if mode == "half":
        return jnp.where(low, up, down)
    even = me % 2 == 0
    return jnp.where(even, up, down) if mode == "even" else jnp.where(even, down, up)


def stage_kernel(spec, *refs):
    order, targets, lane_xor, rows, strip, jobs, right_view, left_views, keep, pack, known, n_after = spec
    ranks, tiles, *refs = refs
    n_right, right_at = right_view
    right, refs = refs[:n_right], refs[n_right:]
    lefts = []
    for number, source, target, length in left_views:
        lefts.append((refs[:number], source, target, length))
        refs = refs[number:]
    n_old = order
    old_left, refs = refs[:n_old], refs[n_old:]
    n_coef = order + (1 if known else 0)
    old_coef, refs = refs[:n_coef], refs[n_coef:]
    refs = refs[n_after:]
    if not known:
        patterns, *refs = refs
    outs, refs = refs[: len(jobs)], refs[len(jobs) :]
    coef_out = pack_out = None
    if keep:
        coef_out, *refs = refs
    if pack:
        pack_out, *refs = refs
    v_all, x_all, l_all, c_all, b_all, v_sem, x_sem, l_sem, c_sem, o_sem = refs

    slots, count, width = c_all.shape[1:]
    tile = l_all.shape[3]
    me, size, low = place()
    which = jnp.where(low, targets - 1 - order, order)

    def v_copies(slot):
        start = 0
        for piece in right:
            height = piece.shape[1]
            yield pltpu.make_async_copy(
                piece.at[slot, :, pl.ds(right_at, tile)], v_all.at[slot, pl.ds(start, height)], v_sem.at[slot]
            )
            start += height

    def x_copy(slot):
        return pltpu.make_async_copy(patterns.at[pl.ds(slot * tile, tile)], x_all.at[slot], x_sem.at[slot])

    def l_copies():
        for pieces, source, target, length in lefts:
            start = 0
            for piece in pieces:
                height = piece.shape[1]
                yield pltpu.make_async_copy(
                    piece.at[:, :, pl.ds(source, length)],
                    l_all.at[order, :, pl.ds(start, height), pl.ds(target, length)],
                    l_sem.at[order],
                )
                start += height

    def old_copies():
        for at in range(n_coef):
            yield pltpu.make_async_copy(old_coef[at], c_all.at[at], c_sem.at[at])
        for at in range(n_old):
            yield pltpu.make_async_copy(old_left[at], l_all.at[at], l_sem.at[at])

    if not known:
        for slot in range(slots):
            for copy in v_copies(slot):
                copy.start()
            x_copy(slot).start()
    for copy in l_copies():
        copy.start()
    for copy in old_copies():
        copy.start()

    pending = []
    if not known:
        part = math.gcd(count, 256)
        for slot in range(slots):
            for copy in v_copies(slot):
                copy.wait()
            x_copy(slot).wait()
            rank = ranks[which, tiles[me * slots + slot]]

            @pl.loop(0, count // part)
            def _(index, slot=slot, rank=rank):
                span = pl.ds(pl.multiple_of(index * part, part), part)
                value = jnp.dot(v_all[slot, span], x_all[slot], preferred_element_type=jnp.float32)
                row = lax.broadcasted_iota(jnp.int32, value.shape, 0) + index * part
                if lane_xor:
                    row = row ^ (lax.axis_index("pat") * lane_xor)
                c_all[order, slot, span] = jnp.where(row < rank, value, 0.0).astype(c_all.dtype)

        if keep:
            pending.append(pltpu.make_async_copy(c_all.at[order], coef_out, o_sem.at[len(jobs)]))
            pending[-1].start()
    for copy in l_copies():
        copy.wait()
    if pack:
        pending.append(pltpu.make_async_copy(l_all.at[order], pack_out, o_sem.at[len(jobs) + 1]))
        pending[-1].start()
    for copy in old_copies():
        copy.wait()

    shift = jnp.where(low, tile - rows, 0)
    for number, (mode, step, first_strip, strips) in enumerate(jobs):
        block = block_of(mode, step)

        @pl.loop(0, strips)
        def _(index, number=number, block=block, first_strip=first_strip):
            first = block * rows + (first_strip + index) * strip
            row = first // tile
            at = jnp.clip(jnp.where(low, targets - 1 - row, row), 0, order)
            start = first % tile
            rolled = jnp.where(start >= shift, start - shift, start - shift + tile)
            start = pl.multiple_of(jnp.where(at == 0, rolled, start), strip)
            value = jnp.zeros((strip, width), jnp.float32)
            for slot in range(slots):
                value = value + lax.dot_general(
                    l_all[at, slot, :, pl.ds(start, strip)],
                    c_all[at, slot],
                    (((0,), (0,)), ((), ())),
                    preferred_element_type=jnp.float32,
                )
            b_all[number, pl.ds(pl.multiple_of(index * strip, strip), strip)] = value.astype(b_all.dtype)

        pending.append(pltpu.make_async_copy(b_all.at[number, pl.ds(0, strips * strip)], outs[number], o_sem.at[number]))
        pending[-1].start()
    for copy in pending:
        copy.wait()


def stage_call(name, order, targets, lane_xor, rows, strip, jobs, right, lefts, old_left, old_coef, patterns, ranks,
               tiles, tile, keep, pack, after=()):
    known = right is None
    pieces, right_at = ([], 0) if known else right
    left_pieces = [piece for group, *_ in lefts for piece in group]
    slots = patterns.shape[0] // tile
    width = patterns.shape[1]
    count = sum(piece.shape[1] for piece in lefts[0][0])
    most = max([strips for *_, strips in jobs])
    out_shape = [jax.ShapeDtypeStruct((strips * strip, width), jnp.bfloat16) for *_, strips in jobs]
    if keep:
        out_shape.append(jax.ShapeDtypeStruct((slots, count, width), jnp.bfloat16))
    if pack:
        out_shape.append(jax.ShapeDtypeStruct((slots, count, tile), jnp.bfloat16))
    operands = [*pieces, *left_pieces, *old_left, *old_coef, *after] + ([] if known else [patterns])
    spec = (order, targets, lane_xor, rows, strip, tuple(jobs), (len(pieces), right_at),
            tuple((len(group), *rest) for group, *rest in lefts), keep, pack, known, len(after))
    total = sum(strips for *_, strips in jobs)
    flops = 2 * slots * count * width * (total * strip + (0 if known else tile))
    moved = 2 * slots * ((order + 2) * count * tile + (0 if known else tile * width) + (order + 1) * count * width)
    small = (1, 8, 128)
    return pl.pallas_call(
        functools.partial(stage_kernel, spec),
        out_shape=out_shape,
        in_specs=[SMEM, SMEM] + [HBM] * len(operands),
        out_specs=[HBM] * len(out_shape),
        scratch_shapes=[
            pltpu.VMEM(small if known else (slots, count, tile), jnp.bfloat16),
            pltpu.VMEM(small if known else (slots, tile, width), jnp.bfloat16),
            pltpu.VMEM((order + 1, slots, count, tile), jnp.bfloat16),
            pltpu.VMEM((order + 1, slots, count, width), jnp.bfloat16),
            pltpu.VMEM((len(jobs), most * strip, width), jnp.bfloat16),
            pltpu.SemaphoreType.DMA((slots,)),
            pltpu.SemaphoreType.DMA((slots,)),
            pltpu.SemaphoreType.DMA((order + 1,)),
            pltpu.SemaphoreType.DMA((order + 1,)),
            pltpu.SemaphoreType.DMA((len(jobs) + 2,)),
        ],
        cost_estimate=pl.CostEstimate(flops=flops, bytes_accessed=moved + 2 * total * strip * width, transcendentals=0),
        name=name,
    )(ranks, tiles, *operands)


def final_kernel(*refs):
    own, one, two, *_, out = refs
    out[...] = own[...].astype(jnp.float32) + one[...].astype(jnp.float32) + two[...].astype(jnp.float32)


def final_call(own, one, two, index, whole):
    rows, width = own.shape
    strip = one.shape[0]
    height = strip // 2
    operands = [own, one, two]
    there = pl.BlockSpec((height, width), lambda r: (2 * index + r, 0))
    here = pl.BlockSpec((height, width), lambda r: (r, 0))
    specs = [there, here, here]
    aliases = {}
    if whole is not None:
        operands.append(whole)
        specs.append(HBM)
        aliases = {3: 0}
    return pl.pallas_call(
        final_kernel,
        out_shape=jax.ShapeDtypeStruct((rows, width), jnp.float32),
        grid=(2,),
        in_specs=specs,
        out_specs=there,
        input_output_aliases=aliases,
        cost_estimate=pl.CostEstimate(flops=2 * strip * width, bytes_accessed=10 * strip * width, transcendentals=0),
        name=f"final_{index}",
    )(*operands)


def swap(value, mask):
    size = lax.axis_size("pat")
    return lax.ppermute(value, "pat", [(at, at ^ mask) for at in range(size)])


def gather(shard, first):
    size = lax.axis_size("pat")
    if size != 8:
        whole = lax.all_gather(shard, "pat", axis=1, tiled=True)
        return [whole], whole
    second = 6 - first
    near = swap(shard, first)
    side = swap(shard, second)
    far = swap(near, second)
    mine = {0: shard, first: near, second: side, first ^ second: far}
    pieces = dict(mine)
    for mask, value in mine.items():
        pieces[mask ^ 1] = swap(value, 1)
    return [pieces[mask] for mask in range(size)], near


def tie(value, *others):
    return lax.optimization_barrier((value, *others))[0]


def body(patterns, left_factors, right_factors, ranks, source_slot_tile):
    targets, slots, rank_cols, tile = left_factors.shape
    me, size, low = place()
    rows = targets * tile // size
    strip = math.gcd(rows, tile)
    strips = rows // strip
    lane_xor = rank_cols if lax.axis_size("pat") == 8 else 0

    def take(array, order):
        target = jnp.where(low, targets - 1 - order, order)
        return lax.dynamic_index_in_dim(array, target, 0, keepdims=False)

    right, left = take(right_factors, 0), take(left_factors, 0)
    left = jnp.where(low, jnp.roll(left, rows - tile, axis=2), left)
    groups, near = gather(jnp.concatenate([right, left[:, :, :strip]], axis=2), 2)
    more, _ = gather(tie(left[:, :, strip:], near), 4)

    plan = [[] for _ in range(targets)]
    for step in range(1, size):
        used = targets - (size - step) * rows // tile
        if 2 * step <= size:
            plan[used - 1].append(("half", step, 0, strips))
        else:
            plan[targets - 1] += [("even", step, 0, strips), ("odd", step, 0, strips)]
    plan[targets - 1].append(("own", 0, 0, strips))

    common = (targets, lane_xor, rows, strip)
    partial = {}
    first_left = (groups, tile, 0, strip)
    head, coef0 = stage_call(
        "stage_first", 0, *common, [("half", 1, 0, 1)], (groups, 0), [first_left], [], [], patterns, ranks,
        source_slot_tile, tile, True, False,
    )
    jobs = [("half", 1, 1, strips - 1)] + plan[0][1:]
    results = stage_call(
        "stage_0", 0, *common, jobs, None, [first_left, (more, 0, strip, tile - strip)], [], [coef0], patterns, ranks,
        source_slot_tile, tile, False, True, after=[head],
    )
    partial["half", 1] = (head, results[0])
    for job, value in zip(jobs[1:], results[1:]):
        partial[job[:2]] = value
    packed, coef = [results[-1]], [coef0]
    latest = results[0]

    joined = []
    for order in range(1, targets):
        shard = jnp.concatenate([take(right_factors, order), take(left_factors, order)], axis=2)
        joined.append(gather(tie(shard, head if order == 1 else latest), 2 if order % 2 else 4)[0])

    one, two = [None] * strips, [None] * strips
    parity = low == (me % 2 == 1)

    def wide(value):
        return value.astype(jnp.float32)

    def send(step, index):
        span = slice(index * strip, (index + 1) * strip)
        if step == 1:
            head, rest = partial["half", 1]
            a = b = head if index == 0 else rest[(index - 1) * strip : index * strip]
        elif 2 * step <= size:
            other = jnp.zeros_like(one[index]) if two[index] is None else two[index]
            value = wide(partial["half", step][span]) + wide(jnp.where(parity, one[index], other))
            a = b = value.astype(jnp.bfloat16)
        else:
            a = (wide(partial["even", step][span]) + wide(two[index])).astype(jnp.bfloat16)
            b = (wide(partial["odd", step][span]) + wide(one[index])).astype(jnp.bfloat16)
        evens = [(at, at ^ 1) for at in range(size)]
        odds = [pair for at in range(1, size - 1, 2) for pair in ((at, at + 1), (at + 1, at))]
        one[index] = lax.ppermute(a, "src", evens)
        if step > 1:
            two[index] = lax.ppermute(b, "src", odds)
        return a

    turn, step = latest, 1
    for order in range(1, targets + 1):
        while step < size and (("half", step) in partial or ("even", step) in partial):
            sent = [send(step, index) for index in range(strips)]
            turn, step = (latest if step == 1 else sent[0]), step + 1
        if order == targets:
            break
        last = order == targets - 1
        results = stage_call(
            f"stage_{order}", order, *common, plan[order], (joined[order - 1], 0), [(joined[order - 1], tile, 0, tile)],
            packed, coef, patterns, ranks, source_slot_tile, tile, not last, not last, after=[turn],
        )
        for job in plan[order]:
            partial[job[:2]], *results = results
        if not last:
            coef.append(results[0])
            packed.append(results[1])
    out = None
    for index in range(strips):
        out = final_call(partial["own", 0], one[index], two[index], index, out)
    return out


def solution(mesh):
    in_specs = (P("src", "pat"), P(None, "src", "pat", None), P(None, "src", "pat", None), P(), P())
    out_specs = P("src", "pat")
    return jax.shard_map(body, mesh=mesh, in_specs=in_specs, out_specs=out_specs, check_vma=False)
```
